256 devices in a mesh: row: 32 (over y, z_hi, core), col: 8 (over z_lo, x).
Axes of the slice: x: 4, y: 4, z: 8 (z_hi: 4, z_lo: 2; z = z_hi * 2 + z_lo), core: 2. Of those that a mesh axis runs over, the one named last changes fastest.
Arguments:
- c_matrix: bfloat16 [8, 768, 6144], P(None, 'row', 'col'), may hold values from -6 to 6
- beta_values: bfloat16 [1, 48, 6, 128, 128], P(None, 'col'), may hold values from -0.21875 to 0.21875
- beta_rows: int32 [1, 48, 6], P(None, 'col'), may hold values from 0 to 47, as said below
- alpha_values: bfloat16 [1, 8, 32, 32, 24, 24], P(None, None, 'row'), may hold values from -0.21875 to 0.21875
- alpha_rows: int32 [1, 8, 32, 32], P(None, None, 'row'), may hold values from 0 to 255, as said below
- gaps: float32 [8, 768, 6144], P(None, 'row', 'col'), may hold values from 0.5 to 4
Outputs:
- update: float32 [8, 768, 6144], P(None, 'row', 'col')
The draws below stay inside these ranges and needn't reach their ends.
Inputs may be any that keep to these rules, and one draw needn't show every extreme that they name: For every k and tile column j, beta_rows[k, j] lists 6 distinct tile rows and its first entry is j. For every k, g, r, alpha_rows[k, g, r] lists 32 distinct tile rows and its first entry is the tile column g * 32 + r.
All inputs are finite; a program needn't handle non-finite values.
Results may differ from the reference program's by a relative error of at most 0.0029.
Values may be sent and summed in bfloat16 or wider, within the bound.
No kernel may reach another device: no remote copies, remote signals or barrier semaphores. Data moves between devices by JAX's collectives and lax.ppermute only.
A program may use at most 128 MiB of HBM per device.

```python
import math
import jax
import jax.numpy as jnp
from jax import lax

ORDER = 6144
PAIRS = 1
TILE_B = 128
GROUPS = 8
SPAN = 768
ATILE = 24
ROWTILES = 32
BTILES = 48
BNZ = 6
ATILES = 256
ANZ = 32


def tile_lists(key, operators, tile_total, listed):
    scores = jax.random.randint(key, (operators, tile_total, tile_total), 0, 1 << 20) * tile_total
    scores = scores + jnp.arange(tile_total, dtype=jnp.int32)
    scores = jnp.where(jnp.eye(tile_total, dtype=bool)[None], -1, scores)
    return jnp.argsort(scores, axis=-1)[..., :listed].astype(jnp.int32)


def draw_beta_rows(key, part):
    return tile_lists(jax.random.fold_in(key, 11), PAIRS, BTILES, BNZ)


def draw_alpha_rows(key, part):
    tile_table = tile_lists(jax.random.fold_in(key, 23), PAIRS, ATILES, ANZ)
    return tile_table.reshape(PAIRS, GROUPS, ROWTILES, ANZ)


def shard_levels(own_key, shape, pieces, low, top_value):
    def one(dim, blocks):
        steps = jax.random.uniform(jax.random.fold_in(jax.random.fold_in(own_key, 6), dim), (blocks,), jnp.float32, low / len(pieces), top_value / len(pieces))
        return jnp.repeat(jnp.exp(steps), shape[dim] // blocks).reshape((-1,) + (1,) * (len(shape) - dim - 1))

    level = one(*pieces[0])
    for cut in pieces[1:]:
        level = level * one(*cut)
    return level


def centred(own_key, shape, spread, reach, pieces=(), kind=jnp.bfloat16):
    drawn = jax.random.normal(own_key, shape, jnp.float32) * spread
    if len(pieces) > 0:
        drawn = shard_levels(own_key, shape, pieces, -0.22, 0.18) * drawn
    return jnp.clip(drawn, min=-reach, max=reach).astype(kind)


def setup_inputs(seed: int = 0) -> dict:
    keys = jax.random.split(jax.random.key(seed), 7)
    return {
        "c_matrix": centred(keys[0], (GROUPS, SPAN, ORDER), 1.0, 6.0, ((1, 32), (2, 8))),
        "beta_values": centred(keys[1], (PAIRS, BTILES, BNZ, TILE_B, TILE_B), (BNZ * TILE_B) ** -0.5, 0.21875, ((1, 8),)),
        "beta_rows": draw_beta_rows(jax.random.fold_in(keys[6], 71), 0),
        "alpha_values": centred(keys[3], (PAIRS, GROUPS, ROWTILES, ANZ, ATILE, ATILE), (ANZ * ATILE) ** -0.5, 0.21875, ((2, 32),)),
        "alpha_rows": draw_alpha_rows(jax.random.fold_in(keys[6], 71), 0),
        "gaps": jnp.clip(jnp.exp(math.log(4.0) - 2.0794415 * jax.random.uniform(keys[5], (GROUPS, SPAN, ORDER), jnp.float32) ** shard_levels(keys[5], (GROUPS, SPAN, ORDER), ((1, 32), (2, 8)), -0.2, 0.2)), 0.5, 4.0),
    }


def reference(c_matrix, beta_values, beta_rows, alpha_values, alpha_rows, gaps):
    c_full = c_matrix.reshape(ORDER, ORDER)
    c_tiled = c_full.reshape(ORDER, BTILES, TILE_B)
    alpha_tiles = alpha_values.reshape(PAIRS, ATILES, ANZ, ATILE, ATILE)
    alpha_lists = alpha_rows.reshape(PAIRS, ATILES, ANZ).astype(jnp.int32)

    def one_pair(summed, inputs):
        beta_tiles, beta_lists, pair_tiles, pair_lists = inputs
        picked = c_tiled[:, beta_lists].astype(jnp.float32)
        product = jnp.einsum("ajzt,jzts->ajs", picked, beta_tiles.astype(jnp.float32))
        rounded = lax.optimization_barrier(product.astype(jnp.bfloat16))
        x_matrix = rounded.astype(jnp.float32).reshape(ATILES, ATILE, ORDER)

        def one_slot(partial_value, slot):
            slot_tiles, slot_rows = slot
            contrib = jnp.einsum("quv,qvn->qun", slot_tiles.astype(jnp.float32), x_matrix)
            return partial_value.at[slot_rows].add(contrib), None

        summed, _ = lax.scan(one_slot, summed, (jnp.moveaxis(pair_tiles, 1, 0), jnp.moveaxis(pair_lists, 1, 0)))
        return summed, None

    start_sum = jnp.zeros((ATILES, ATILE, ORDER), jnp.float32)
    summed, _ = lax.scan(one_pair, start_sum, (beta_values, beta_rows.astype(jnp.int32), alpha_tiles, alpha_lists))
    y_matrix = summed.reshape(ORDER, ORDER)
    sigma = y_matrix + y_matrix.T
    return (sigma / gaps.reshape(ORDER, ORDER)).reshape(GROUPS, SPAN, ORDER)
```

```python
import jax
import jax.numpy as jnp
from jax import lax
from jax.experimental import pallas as pl
from jax.experimental.pallas import tpu as pltpu
from jax.sharding import Mesh, PartitionSpec as P

BF = jnp.bfloat16
F32 = jnp.float32
NY, NZ, NC, NL, NX = 4, 4, 2, 2, 4
NH = NZ * NC
G, U, RT = 8, 24, 32
ROWS = G * U
COLS = 768
PART = COLS // NH
STEPS = (0, 1, -1, 2)
HBM = pl.BlockSpec(memory_space=pltpu.HBM)
VM = pl.BlockSpec(memory_space=pltpu.VMEM)
SM = pl.BlockSpec(memory_space=pltpu.SMEM)


def shift_x(a, k):
    return lax.ppermute(a, "x", [(i, (i + k) % NX) for i in range(NX)])


def flip_zl(a):
    return lax.ppermute(a, "zl", [(0, 1), (1, 0)])


def flip_core(a):
    return lax.ppermute(a, "core", [(0, 1), (1, 0)])


def shift_y(a, k):
    return lax.ppermute(a, "y", [(i, (i + k) % NY) for i in range(NY)])


def cross_z(a):
    moves = []
    for zh in range(NZ):
        moves.append((zh * 2, (zh - 1) % NZ * 2 + 1))
        moves.append((zh * 2 + 1, (zh + 1) % NZ * 2))
    return lax.ppermute(a, ("zh", "zl"), moves)


def send_step(a, label):
    moves = []
    for zh in range(NZ):
        for zl in range(NL):
            to = (zh + (1 - 2 * zl) * STEPS[label]) % NZ
            moves.append((zh * 2 + zl, to * 2 + zl))
    return lax.ppermute(a, ("zh", "zl"), moves)


def exchange(payloads):
    direct = [payloads[0]] + [send_step(payloads[k], k) for k in range(1, NZ)]
    return direct + [flip_core(a) for a in direct]


def pack(pieces):
    lane = lax.broadcasted_iota(jnp.int32, pieces[0].shape, 1)
    p0, r1, r2, r3 = pieces[0], *(pltpu.roll(pieces[i], 128 - 32 * i, 1) for i in (1, 2, 3))
    return jnp.concatenate(
        [
            jnp.where(lane < 96, p0, r1),
            jnp.where(lane < 64, r1, r2),
            jnp.where(lane < 32, r2, r3),
        ],
        axis=1,
    )


def unpack(packed):
    t0, t1, t2 = (packed[:, i * 128 : (i + 1) * 128] for i in range(3))
    lane = lax.broadcasted_iota(jnp.int32, t0.shape, 1)
    return [
        t0,
        pltpu.roll(jnp.where(lane < 96, t1, t0), 32, 1),
        pltpu.roll(jnp.where(lane < 64, t2, t1), 64, 1),
        pltpu.roll(t2, 96, 1),
    ]


def gather_c(own):
    over, left, right = flip_zl(own), shift_x(own, 1), shift_x(own, -1)
    over_right, far, over_left = shift_x(over, -1), shift_x(left, 1), flip_zl(left)
    over_far = shift_x(over_right, -1)
    return [own, right, far, left, over, over_right, over_far, over_left]


def x_kernel(slots, *refs):
    blocks, (b_ref, perm_ref), outs = refs[:8], refs[8:10], refs[10 : 10 + NZ]
    cbuf, xs, sems = refs[10 + NZ :]
    copies = [pltpu.make_async_copy(blocks[k], cbuf.at[k], sems.at[k]) for k in range(8)]
    for cp in copies:
        cp.start()
    for cp in copies:
        cp.wait()
    for j in range(6):
        picked = []
        for z in range(6):
            slot = slots[j * 6 + z]
            k, t = slot // 6, slot % 6
            picked.append(cbuf[k, :, pl.ds(pl.multiple_of(t * 128, 128), 128)])
        lhs = jnp.concatenate(picked, axis=1)
        xs[:, j * 128 : (j + 1) * 128] = jnp.dot(
            lhs, b_ref[j], preferred_element_type=F32
        ).astype(BF)
    for label in range(NH):
        piece = jnp.dot(
            xs[...], perm_ref[:, label * 128 : (label + 1) * 128], preferred_element_type=F32
        )
        outs[label // 2][label % 2] = pack([piece[i * 48 : (i + 1) * 48] for i in range(4)]).astype(BF)


def a_kernel(lists, *refs):
    ps, xs, (own_ref, s1, s2, s3) = refs[:8], refs[8:16], refs[16:20]
    acc, pbuf, xbuf, res, psem, xsem = refs[20:]
    pc, xc = [], []
    for i in range(NH):
        pc.append(pltpu.make_async_copy(ps[i].at[pl.ds(0, ROWS)], pbuf.at[i], psem.at[i]))
        xc.append(pltpu.make_async_copy(xs[i % 2 * NZ + i // 2].at[i % 2], xbuf.at[i], xsem.at[i]))
    for cp in pc + xc:
        cp.start()
    acc[...] = jnp.zeros_like(acc)
    for cp in pc + xc:
        cp.wait()
    rows = lax.broadcasted_iota(jnp.int32, (ROWS, 128), 0)
    blank = jnp.zeros((64, 256), F32)

    @pl.loop(0, NH)
    def _(label):
        x = jnp.concatenate(unpack(xbuf[label].astype(F32)), axis=0)
        for pair in range(4):
            sides = []
            for g in (2 * pair, 2 * pair + 1):
                keep = (rows >= g * U) & (rows < (g + 1) * U)
                sides.append(jnp.where(keep, x, 0.0))
            diag = jnp.concatenate(sides, axis=1)
            even = jnp.concatenate([diag, blank], axis=0).astype(BF)
            odd = jnp.concatenate([blank, diag], axis=0).astype(BF)
            for q in range(4):
                first = q * ROWS - q % 2 * 64
                res[pair % 2, q * ROWS : (q + 1) * ROWS] = jnp.dot(
                    pbuf[label, :, first : first + 256],
                    odd if q % 2 else even,
                    preferred_element_type=F32,
                )
            for side in range(2):
                g = 2 * pair + side
                for batch in range(4):
                    spots, sums = [], []
                    for z in range(batch * 8, batch * 8 + 8):
                        t = lists[label * (G * RT) + g * RT + z]
                        spot = pl.ds(pl.multiple_of(t * U, 8), U)
                        spots.append(spot)
                        sums.append(
                            acc[spot, :]
                            + res[pair % 2, z * U : (z + 1) * U, side * 128 : (side + 1) * 128]
                        )
                    for spot, total in zip(spots, sums):
                        acc[spot, :] = total

    size = ROWS * NH
    own_ref[...] = acc[0:size]
    quarter = size // 4
    for k, ref in enumerate((s1, s2, s3)):
        first = (k + 1) * size
        ref[...] = pack(
            [acc[first + i * quarter : first + (i + 1) * quarter] for i in range(4)]
        ).astype(BF)


def y_kernel(dests, own, r1, r2, r3, ident, *refs):
    ds, m_ref, y = refs[:NZ], refs[NZ], refs[NZ + 1]
    quarter = ROWS * NH // 4
    parts = [unpack(r[...].astype(F32)) for r in (r1, r2, r3)]
    for i in range(4):
        span = slice(i * quarter, (i + 1) * quarter)
        y[span, :] = own[span, :] + parts[0][i] + parts[1][i] + parts[2][i]
    for label in range(NH):
        h = dests[label]
        pieces = []
        for g in range(G):
            pieces.append(y[pl.ds(pl.multiple_of((g * NH + h) * U, 8), U), :])
        pairs = [jnp.concatenate(pieces[2 * i : 2 * i + 2], axis=0) for i in range(4)]
        ds[label // 2][label % 2] = pack(pairs).astype(BF)
    for g in range(G):
        block = y[g * ROWS : (g + 1) * ROWS, :].astype(BF)
        turned = lax.dot_general(
            ident[...], block, (((1,), (1,)), ((), ())), preferred_element_type=F32
        )
        for ys in range(NY):
            m_ref[ys * G + g] = turned[ys * U : (ys + 1) * U, :].astype(BF)


def out_kernel(*refs):
    ds, (m_ref, perm_ref, gaps, out_ref) = refs[:NH], refs[NH:]
    total = jnp.zeros((ROWS, COLS), F32)
    for label in range(NH):
        packed = ds[label % 2 * NZ + label // 2][label % 2].astype(F32)
        piece = jnp.concatenate(unpack(packed), axis=0).astype(BF)
        total = total + jnp.dot(piece, perm_ref[label], preferred_element_type=F32)
    row = lax.broadcasted_iota(jnp.int32, (ROWS, COLS), 0)
    col = lax.broadcasted_iota(jnp.int32, (ROWS, COLS), 1)
    for ys in range(NY):
        place = jnp.where(col == row + ys * ROWS, 1.0, 0.0).astype(BF)
        total = total + jnp.dot(m_ref[ys], place, preferred_element_type=F32)
    out_ref[...] = total / gaps[...]


def params():
    return pltpu.CompilerParams(vmem_limit_bytes=50 * 1024 * 1024)


def per_device(c_matrix, beta_values, beta_rows, alpha_values, alpha_rows, gaps):
    y, zh, core = lax.axis_index("y"), lax.axis_index("zh"), lax.axis_index("core")
    zl, x = lax.axis_index("zl"), lax.axis_index("x")
    sign = 1 - 2 * zl
    steps = jnp.array([s for s in STEPS for _ in range(NC)], jnp.int32)
    flips = jnp.array([0, 1] * NZ, jnp.int32)
    h_to = (zh + sign * steps) % NZ * NC + (core ^ flips)
    h_from = (zh - sign * steps) % NZ * NC + (core ^ flips)

    tiles = alpha_values[0, :, 0].reshape(G, 4, 8, U, U)
    tiles = jnp.transpose(tiles, (2, 3, 1, 0, 4)).reshape(ROWS, COLS)
    listed = jnp.pad(alpha_rows[0, :, 0].astype(BF).reshape(1, G * RT), ((0, 7), (0, COLS - G * RT)))
    tiles = jnp.concatenate([tiles, listed], axis=0)
    near = cross_z(tiles)
    next_ = flip_zl(near)
    far = cross_z(next_)
    a_parts = []
    for part in (tiles, near, next_, far):
        a_parts += [part, flip_core(part)]
    lists = jnp.stack([a[ROWS, : G * RT] for a in a_parts]).astype(jnp.int32)
    tile_row = lists % RT
    lists = ((tile_row // NH - y) % NY) * (G * NH) + lists // RT * NH + tile_row % NH

    blocks = gather_c(c_matrix.reshape(ROWS, COLS))
    col_block = beta_rows[0] // 6
    slots = (((col_block // NX) ^ zl) * NX + (col_block % NX - x) % NX) * 6 + beta_rows[0] % 6
    lane = jnp.arange(128, dtype=jnp.int32)
    place = jnp.where(lane < PART, lane // U * (NH * U) + lane % U, -COLS)
    cols = jnp.arange(COLS, dtype=jnp.int32)
    spread_to = (place[None, :] + h_to[:, None] * U).reshape(-1)
    perm_to = (cols[:, None] == spread_to[None, :]).astype(BF)
    perm_from = (cols[None, None, :] == (place[None, :] + h_from[:, None] * U)[:, :, None]).astype(BF)
    piece = jax.ShapeDtypeStruct((NC, ROWS // 4, 384), BF)
    x_out = pl.pallas_call(
        x_kernel,
        out_shape=[piece] * NZ,
        in_specs=[SM] + [HBM] * 8 + [VM] * 2,
        out_specs=[VM] * NZ,
        scratch_shapes=[
            pltpu.VMEM((8, ROWS, COLS), BF),
            pltpu.VMEM((ROWS, COLS), BF),
            pltpu.SemaphoreType.DMA((8,)),
        ],
        compiler_params=params(),
        name="beta_product",
    )(slots.reshape(-1), *blocks, beta_values[0].reshape(6, 768, 128), perm_to)
    x_parts = exchange(x_out)

    size = ROWS * NH
    part = jax.ShapeDtypeStruct((size // 4, 384), BF)
    own, s1, s2, s3 = pl.pallas_call(
        a_kernel,
        out_shape=[jax.ShapeDtypeStruct((size, 128), F32), part, part, part],
        in_specs=[SM] + [HBM] * 16,
        out_specs=[VM] * 4,
        scratch_shapes=[
            pltpu.VMEM((size * NY, 128), F32),
            pltpu.VMEM((NH, ROWS, COLS), BF),
            pltpu.VMEM((NH, ROWS // 4, 384), BF),
            pltpu.VMEM((2, RT * U, 256), F32),
            pltpu.SemaphoreType.DMA((NH,)),
            pltpu.SemaphoreType.DMA((NH,)),
        ],
        compiler_params=params(),
        name="alpha_product",
    )(lists.reshape(-1), *a_parts, *x_parts)
    r1, r2, r3 = shift_y(s1, 1), shift_y(s2, 2), shift_y(s3, 3)

    y_out = pl.pallas_call(
        y_kernel,
        out_shape=[piece] * NZ + [jax.ShapeDtypeStruct((NY * G, U, ROWS), BF)],
        in_specs=[SM] + [VM] * 5,
        out_specs=[VM] * (NZ + 1),
        scratch_shapes=[pltpu.VMEM((size, 128), F32)],
        compiler_params=params(),
        name="y_sum",
    )(h_to, own, r1, r2, r3, jnp.eye(128, dtype=BF))
    mirrored = lax.all_to_all(y_out[NZ], ("y", "zl", "x"), split_axis=0, concat_axis=0, tiled=True)
    d_parts = exchange(y_out[:NZ])
    out = pl.pallas_call(
        out_kernel,
        out_shape=jax.ShapeDtypeStruct((ROWS, COLS), F32),
        in_specs=[VM] * (NH + 3),
        out_specs=VM,
        compiler_params=params(),
        name="combine",
    )(*d_parts, mirrored.reshape(NY, ROWS, ROWS), perm_from, gaps.reshape(ROWS, COLS))
    return out.reshape(gaps.shape)


def solution(mesh):
    fine = Mesh(mesh.devices.reshape(NY, NZ, NC, NL, NX), ("y", "zh", "core", "zl", "x"))
    row, col = ("y", "zh", "core"), ("zl", "x")
    placed = (
        P(None, row, col),
        P(None, col, None, None, None),
        P(None, col, None),
        P(None, None, row, None, None, None),
        P(None, None, row, None),
        P(None, row, col),
    )
    return jax.shard_map(
        per_device, mesh=fine, in_specs=placed, out_specs=P(None, row, col), check_vma=False
    )
```

```python
import jax
import jax.numpy as jnp
import numpy as np
from jax import lax
from jax.experimental import pallas as pl
from jax.experimental.pallas import tpu as pltpu
from jax.sharding import Mesh, PartitionSpec as P

BF = jnp.bfloat16
F32 = jnp.float32
NY, NZ, NC, NL, NX = 4, 4, 2, 2, 4
NH = NZ * NC
G, U, RT = 8, 24, 32
ROWS = G * U
COLS = 768
PART = COLS // NH
STEPS = (0, 1, -1, 2)
HBM = pl.BlockSpec(memory_space=pltpu.HBM)
VM = pl.BlockSpec(memory_space=pltpu.VMEM)
SM = pl.BlockSpec(memory_space=pltpu.SMEM)


def shift_x(a, k):
    return lax.ppermute(a, "x", [(i, (i + k) % NX) for i in range(NX)])


def flip_zl(a):
    return lax.ppermute(a, "zl", [(0, 1), (1, 0)])


def flip_core(a):
    return lax.ppermute(a, "core", [(0, 1), (1, 0)])


def shift_y(a, k):
    return lax.ppermute(a, "y", [(i, (i + k) % NY) for i in range(NY)])


def cross_z(a, step):
    moves = []
    for zh in range(NZ):
        moves.append((zh * 2, (zh - step) % NZ * 2 + 1))
        moves.append((zh * 2 + 1, (zh + step) % NZ * 2))
    return lax.ppermute(a, ("zh", "zl"), moves)


def send_step(a, label):
    moves = []
    for zh in range(NZ):
        for zl in range(NL):
            to = (zh + (1 - 2 * zl) * STEPS[label]) % NZ
            moves.append((zh * 2 + zl, to * 2 + zl))
    return lax.ppermute(a, ("zh", "zl"), moves)


def exchange(payloads):
    direct = [payloads[0]] + [send_step(payloads[k], k) for k in range(1, NZ)]
    return direct + [flip_core(a) for a in direct]


def pack(pieces):
    lane = lax.broadcasted_iota(jnp.int32, pieces[0].shape, 1)
    p0, r1, r2, r3 = pieces[0], *(pltpu.roll(pieces[i], 128 - 32 * i, 1) for i in (1, 2, 3))
    return jnp.concatenate(
        [
            jnp.where(lane < 96, p0, r1),
            jnp.where(lane < 64, r1, r2),
            jnp.where(lane < 32, r2, r3),
        ],
        axis=1,
    )


def unpack(packed):
    t0, t1, t2 = (packed[:, i * 128 : (i + 1) * 128] for i in range(3))
    lane = lax.broadcasted_iota(jnp.int32, t0.shape, 1)
    return [
        t0,
        pltpu.roll(jnp.where(lane < 96, t1, t0), 32, 1),
        pltpu.roll(jnp.where(lane < 64, t2, t1), 64, 1),
        pltpu.roll(t2, 96, 1),
    ]


def x_kernel(slots, *refs):
    blocks, (b_ref, perm_ref), outs = refs[:8], refs[8:10], refs[10 : 10 + NZ]
    cbuf, xs, sems = refs[10 + NZ :]
    copies = [pltpu.make_async_copy(blocks[k], cbuf.at[k], sems.at[k]) for k in range(8)]
    for cp in copies:
        cp.start()
    for cp in copies:
        cp.wait()
    for j in range(6):
        picked = []
        for z in range(6):
            slot = slots[j * 6 + z]
            k, t = slot // 6, slot % 6
            picked.append(cbuf[k, :, pl.ds(pl.multiple_of(t * 128, 128), 128)])
        lhs = jnp.concatenate(picked, axis=1)
        xs[:, j * 128 : (j + 1) * 128] = jnp.dot(
            lhs, b_ref[j], preferred_element_type=F32
        ).astype(BF)
    for label in range(NH):
        piece = jnp.dot(
            xs[...], perm_ref[:, label * 128 : (label + 1) * 128], preferred_element_type=F32
        )
        outs[label // 2][label % 2] = pack([piece[i * 48 : (i + 1) * 48] for i in range(4)]).astype(BF)


def turn_rows():
    turn = np.zeros((RT * U, RT * U), np.float32)
    for z in range(RT):
        for u in range(U):
            turn[z * U + u, u * RT + z] = 1.0
    return jnp.asarray(turn, BF)


def tiles_kernel(values, rows, turn, out, wide):
    for g in range(G):
        for q in range(U // 4):
            wide[g * U : (g + 1) * U, q * 128 : (q + 1) * 128] = jnp.concatenate(
                [values[g, 4 * q + i].astype(F32) for i in range(4)], axis=1
            )
    flat = wide[...]
    blank = jnp.zeros((64, COLS), F32)
    even = jnp.concatenate([flat, blank], axis=0).astype(BF)
    odd = jnp.concatenate([blank, flat], axis=0).astype(BF)
    for q in range(4):
        turned = lax.dot_general(
            turn[q * ROWS : (q + 1) * ROWS, :],
            odd if q % 2 else even,
            (((1,), (1,)), ((), ())),
            preferred_element_type=F32,
        )
        if q % 2 == 0:
            kept = turned
        else:
            first = (q - 1) * ROWS
            out[:ROWS, first : first + 128] = kept[:, :128].astype(BF)
            out[:ROWS, first + 128 : first + 256] = (kept[:, 128:] + turned[:, :128]).astype(BF)
            out[:ROWS, first + 256 : first + 384] = turned[:, 128:].astype(BF)
    tile_rows = rows[...].astype(F32)
    line = [
        jnp.concatenate([tile_rows[4 * k + i : 4 * k + i + 1] for i in range(4)], axis=1)
        for k in range(2)
    ]
    line = jnp.concatenate(line + [jnp.zeros((1, COLS - G * RT), F32)], axis=1)
    out[ROWS:, :] = jnp.broadcast_to(line, (8, COLS)).astype(BF)


def stack_kernel(after, *refs):
    parts, out, sems = refs[:NZ], refs[NZ], refs[NZ + 1]
    copies = [pltpu.make_async_copy(parts[i], out.at[i], sems.at[i]) for i in range(NZ)]
    for cp in copies:
        cp.start()
    for cp in copies:
        cp.wait()


def a_kernel(place, *refs):
    ps, xs, (own_ref, s1, s2, s3) = refs[:2], refs[2:10], refs[10:14]
    acc, pbuf, xbuf, res, spots_v, lists, psem, xsem, lsem = refs[14:]
    pc, xc = [], []
    for i in range(NH):
        k = i % 2 * NZ + i // 2
        pc.append(pltpu.make_async_copy(ps[i % 2].at[i // 2], pbuf.at[i], psem.at[i]))
        xc.append(pltpu.make_async_copy(xs[k].at[i % 2], xbuf.at[i], xsem.at[i]))
    for cp in pc + xc:
        cp.start()
    acc[...] = jnp.zeros_like(acc)
    for cp in pc:
        cp.wait()
    for i in range(NH):
        tile = pbuf[i, ROWS:, : G * RT].astype(F32)[0:1].astype(jnp.int32)
        to_y = ((tile >> 3) - place[0]) & (NY - 1)
        spots_v[i : i + 1] = (to_y * (G * NH) + (tile >> 5) * NH + (tile & 7)) * U
    to_smem = pltpu.make_async_copy(spots_v, lists, lsem)
    to_smem.start()
    for cp in xc:
        cp.wait()
    to_smem.wait()
    rows = lax.broadcasted_iota(jnp.int32, (ROWS, 128), 0)
    blank = jnp.zeros((64, 256), F32)

    @pl.loop(0, NH)
    def _(label):
        x = jnp.concatenate(unpack(xbuf[label].astype(F32)), axis=0)
        for pair in range(4):
            sides = []
            for g in (2 * pair, 2 * pair + 1):
                keep = (rows >= g * U) & (rows < (g + 1) * U)
                sides.append(jnp.where(keep, x, 0.0))
            diag = jnp.concatenate(sides, axis=1)
            even = jnp.concatenate([diag, blank], axis=0).astype(BF)
            odd = jnp.concatenate([blank, diag], axis=0).astype(BF)
            for q in range(4):
                first = q * ROWS - q % 2 * 64
                res[pair % 2, q * ROWS : (q + 1) * ROWS] = jnp.dot(
                    pbuf[label, :ROWS, first : first + 256],
                    odd if q % 2 else even,
                    preferred_element_type=F32,
                )
            for side in range(2):
                g = 2 * pair + side
                for batch in range(4):
                    spots, sums = [], []
                    for z in range(batch * 8, batch * 8 + 8):
                        spot = pl.ds(pl.multiple_of(lists[label, g * RT + z], 8), U)
                        spots.append(spot)
                        sums.append(
                            acc[spot, :]
                            + res[pair % 2, z * U : (z + 1) * U, side * 128 : (side + 1) * 128]
                        )
                    for spot, total in zip(spots, sums):
                        acc[spot, :] = total

    size = ROWS * NH
    own_ref[...] = acc[0:size]
    quarter = size // 4
    for k, ref in enumerate((s1, s2, s3)):
        first = (k + 1) * size
        ref[...] = pack(
            [acc[first + i * quarter : first + (i + 1) * quarter] for i in range(4)]
        ).astype(BF)


def y_kernel(dests, own, r1, r2, r3, ident, *refs):
    ds, m_ref, y = refs[:NZ], refs[NZ], refs[NZ + 1]
    quarter = ROWS * NH // 4
    parts = [unpack(r[...].astype(F32)) for r in (r1, r2, r3)]
    for i in range(4):
        span = slice(i * quarter, (i + 1) * quarter)
        y[span, :] = own[span, :] + parts[0][i] + parts[1][i] + parts[2][i]
    for label in range(NH):
        h = dests[label]
        pieces = []
        for g in range(G):
            pieces.append(y[pl.ds(pl.multiple_of((g * NH + h) * U, 8), U), :])
        pairs = [jnp.concatenate(pieces[2 * i : 2 * i + 2], axis=0) for i in range(4)]
        ds[label // 2][label % 2] = pack(pairs).astype(BF)
    for g in range(G):
        block = y[g * ROWS : (g + 1) * ROWS, :].astype(BF)
        turned = lax.dot_general(
            ident[...], block, (((1,), (1,)), ((), ())), preferred_element_type=F32
        )
        for ys in range(NY):
            m_ref[ys * G + g] = turned[ys * U : (ys + 1) * U, :].astype(BF)


def out_kernel(*refs):
    ds, (m_ref, perm_ref, gaps, out_ref) = refs[:NH], refs[NH:]
    total = jnp.zeros((ROWS, COLS), F32)
    for label in range(NH):
        packed = ds[label % 2 * NZ + label // 2][label % 2].astype(F32)
        piece = jnp.concatenate(unpack(packed), axis=0).astype(BF)
        total = total + jnp.dot(piece, perm_ref[label], preferred_element_type=F32)
    row = lax.broadcasted_iota(jnp.int32, (ROWS, COLS), 0)
    col = lax.broadcasted_iota(jnp.int32, (ROWS, COLS), 1)
    for ys in range(NY):
        place = jnp.where(col == row + ys * ROWS, 1.0, 0.0).astype(BF)
        total = total + jnp.dot(m_ref[ys], place, preferred_element_type=F32)
    out_ref[...] = total / gaps[...]


def params(mib):
    return pltpu.CompilerParams(vmem_limit_bytes=mib * 1024 * 1024)


def per_device(c_matrix, beta_values, beta_rows, alpha_values, alpha_rows, gaps):
    y, zh, core = lax.axis_index("y"), lax.axis_index("zh"), lax.axis_index("core")
    zl, x = lax.axis_index("zl"), lax.axis_index("x")
    sign = 1 - 2 * zl
    steps = jnp.array([s for s in STEPS for _ in range(NC)], jnp.int32)
    flips = jnp.array([0, 1] * NZ, jnp.int32)
    h_to = (zh + sign * steps) % NZ * NC + (core ^ flips)
    h_from = (zh - sign * steps) % NZ * NC + (core ^ flips)

    c_own = c_matrix.reshape(ROWS, COLS)
    over, left, right = flip_zl(c_own), shift_x(c_own, 1), shift_x(c_own, -1)
    over_right, far, over_left = shift_x(over, -1), shift_x(left, 1), shift_x(over, 1)
    over_far = shift_x(over_right, -1)
    blocks = [c_own, right, far, left, over, over_right, over_far, over_left]

    tiles = pl.pallas_call(
        tiles_kernel,
        out_shape=jax.ShapeDtypeStruct((ROWS + 8, COLS), BF),
        in_specs=[VM] * 3,
        out_specs=VM,
        scratch_shapes=[pltpu.VMEM((ROWS, COLS), F32)],
        compiler_params=params(12),
        name="arrange_tiles",
    )(jnp.transpose(alpha_values[0, :, 0], (0, 2, 3, 1)), alpha_rows[0, :, 0], turn_rows())
    a_near = [tiles, cross_z(tiles, 1), send_step(tiles, 2), cross_z(tiles, 2)]

    col_block = beta_rows[0] // 6
    slots = (((col_block // NX) ^ zl) * NX + (col_block % NX - x) % NX) * 6 + beta_rows[0] % 6
    lane = jnp.arange(128, dtype=jnp.int32)
    place = jnp.where(lane < PART, lane // U * (NH * U) + lane % U, -COLS)
    cols = jnp.arange(COLS, dtype=jnp.int32)
    spread_to = (place[None, :] + h_to[:, None] * U).reshape(-1)
    perm_to = (cols[:, None] == spread_to[None, :]).astype(BF)
    perm_from = (cols[None, None, :] == (place[None, :] + h_from[:, None] * U)[:, :, None]).astype(BF)
    piece = jax.ShapeDtypeStruct((NC, ROWS // 4, 384), BF)
    x_out = pl.pallas_call(
        x_kernel,
        out_shape=[piece] * NZ,
        in_specs=[SM, HBM] + [VM] * 9,
        out_specs=[VM] * NZ,
        scratch_shapes=[
            pltpu.VMEM((8, ROWS, COLS), BF),
            pltpu.VMEM((ROWS, COLS), BF),
            pltpu.SemaphoreType.DMA((8,)),
        ],
        compiler_params=params(12),
        name="beta_product",
    )(slots.reshape(-1), pltpu.with_memory_space_constraint(c_own, pltpu.HBM), *blocks[1:], beta_values[0].reshape(6, 768, 128), perm_to)
    x_parts = exchange(x_out)
    a_own = pl.pallas_call(
        stack_kernel,
        out_shape=jax.ShapeDtypeStruct((NZ, ROWS + 8, COLS), BF),
        in_specs=[HBM] * 5,
        out_specs=HBM,
        scratch_shapes=[pltpu.SemaphoreType.DMA((NZ,))],
        compiler_params=params(4),
        name="stack_tiles",
    )(x_out[0], *a_near)

    size = ROWS * NH
    part = jax.ShapeDtypeStruct((size // 4, 384), BF)
    own, s1, s2, s3 = pl.pallas_call(
        a_kernel,
        out_shape=[jax.ShapeDtypeStruct((size, 128), F32), part, part, part],
        in_specs=[SM] + [HBM] * 10,
        out_specs=[VM] * 4,
        scratch_shapes=[
            pltpu.VMEM((size * NY, 128), F32),
            pltpu.VMEM((NH, ROWS + 8, COLS), BF),
            pltpu.VMEM((NH, ROWS // 4, 384), BF),
            pltpu.VMEM((2, RT * U, 256), F32),
            pltpu.VMEM((NH, G * RT), jnp.int32),
            pltpu.SMEM((NH, G * RT), jnp.int32),
            pltpu.SemaphoreType.DMA((NH,)),
            pltpu.SemaphoreType.DMA((NH,)),
            pltpu.SemaphoreType.DMA,
        ],
        compiler_params=params(16),
        name="alpha_product",
    )(y.reshape(1), a_own, flip_core(a_own), *x_parts)
    r2, r1, r3 = shift_y(s2, 2), shift_y(s1, 1), shift_y(s3, 3)

    y_out = pl.pallas_call(
        y_kernel,
        out_shape=[piece] * NZ + [jax.ShapeDtypeStruct((NY * G, U, ROWS), BF)],
        in_specs=[SM] + [VM] * 5,
        out_specs=[VM] * (NZ + 1),
        scratch_shapes=[pltpu.VMEM((size, 128), F32)],
        compiler_params=params(12),
        name="y_sum",
    )(h_to, own, r1, r2, r3, jnp.eye(128, dtype=BF))
    mirrored = lax.all_to_all(y_out[NZ], ("y", "zl", "x"), split_axis=0, concat_axis=0, tiled=True)
    d_parts = exchange(y_out[:NZ])
    out = pl.pallas_call(
        out_kernel,
        out_shape=jax.ShapeDtypeStruct((ROWS, COLS), F32),
        in_specs=[VM] * (NH + 3),
        out_specs=VM,
        compiler_params=params(12),
        name="combine",
    )(*d_parts, mirrored.reshape(NY, ROWS, ROWS), perm_from, gaps.reshape(ROWS, COLS))
    return out.reshape(gaps.shape)


def solution(mesh):
    fine = Mesh(mesh.devices.reshape(NY, NZ, NC, NL, NX), ("y", "zh", "core", "zl", "x"))
    row, col = ("y", "zh", "core"), ("zl", "x")
    placed = (
        P(None, row, col),
        P(None, col, None, None, None),
        P(None, col, None),
        P(None, None, row, None, None, None),
        P(None, None, row, None),
        P(None, row, col),
    )
    return jax.shard_map(
        per_device, mesh=fine, in_specs=placed, out_specs=P(None, row, col), check_vma=False
    )
```

```python
import jax
import jax.numpy as jnp
import numpy as np
from jax import lax
from jax.experimental import pallas as pl
from jax.experimental.pallas import tpu as pltpu
from jax.sharding import Mesh, PartitionSpec as P

BF = jnp.bfloat16
F32 = jnp.float32
NY, NZ, NC, NL, NX = 4, 4, 2, 2, 4
NH = NZ * NC
G, U, RT = 8, 24, 32
ROWS = G * U
COLS = 768
PART = COLS // NH
FIRST = 6
ARRIVAL = (4, 6, 5, 7, 3, 2, 1, 0)
STEPS = (0, 1, -1, 2)
HBM = pl.BlockSpec(memory_space=pltpu.HBM)
VM = pl.BlockSpec(memory_space=pltpu.VMEM)
SM = pl.BlockSpec(memory_space=pltpu.SMEM)


def shift_x(a, k):
    return lax.ppermute(a, "x", [(i, (i + k) % NX) for i in range(NX)])


def flip_zl(a):
    return lax.ppermute(a, "zl", [(0, 1), (1, 0)])


def flip_core(a):
    return lax.ppermute(a, "core", [(0, 1), (1, 0)])


def shift_y(a, k):
    return lax.ppermute(a, "y", [(i, (i + k) % NY) for i in range(NY)])


def cross_z(a, step):
    moves = []
    for zh in range(NZ):
        moves.append((zh * 2, (zh - step) % NZ * 2 + 1))
        moves.append((zh * 2 + 1, (zh + step) % NZ * 2))
    return lax.ppermute(a, ("zh", "zl"), moves)


def send_step(a, label):
    moves = []
    for zh in range(NZ):
        for zl in range(NL):
            to = (zh + (1 - 2 * zl) * STEPS[label]) % NZ
            moves.append((zh * 2 + zl, to * 2 + zl))
    return lax.ppermute(a, ("zh", "zl"), moves)


def pack(pieces):
    lane = lax.broadcasted_iota(jnp.int32, pieces[0].shape, 1)
    p0, r1, r2, r3 = pieces[0], *(pltpu.roll(pieces[i], 128 - 32 * i, 1) for i in (1, 2, 3))
    return jnp.concatenate(
        [
            jnp.where(lane < 96, p0, r1),
            jnp.where(lane < 64, r1, r2),
            jnp.where(lane < 32, r2, r3),
        ],
        axis=1,
    )


def unpack(packed):
    t0, t1, t2 = (packed[:, i * 128 : (i + 1) * 128] for i in range(3))
    lane = lax.broadcasted_iota(jnp.int32, t0.shape, 1)
    return [
        t0,
        pltpu.roll(jnp.where(lane < 96, t1, t0), 32, 1),
        pltpu.roll(jnp.where(lane < 64, t2, t1), 64, 1),
        pltpu.roll(t2, 96, 1),
    ]


def x_kernel(slots, *refs):
    blocks, (b_ref, perm_ref), outs = refs[:8], refs[8:10], refs[10 : 10 + NZ]
    cbuf, xs, sems = refs[10 + NZ :]
    copies = [pltpu.make_async_copy(blocks[i], cbuf.at[k], sems.at[i]) for i, k in enumerate(ARRIVAL)]
    for cp in copies:
        cp.start()
    for cp in copies:
        cp.wait()
    for j in range(6):
        picked = []
        for z in range(6):
            slot = slots[j * 6 + z]
            k, t = slot // 6, slot % 6
            picked.append(cbuf[k, :, pl.ds(pl.multiple_of(t * 128, 128), 128)])
        lhs = jnp.concatenate(picked, axis=1)
        xs[:, j * 128 : (j + 1) * 128] = jnp.dot(
            lhs, b_ref[j], preferred_element_type=F32
        ).astype(BF)
    for label in range(NH):
        piece = jnp.dot(
            xs[...], perm_ref[:, label * 128 : (label + 1) * 128], preferred_element_type=F32
        )
        outs[label // 2][label % 2] = pack([piece[i * 48 : (i + 1) * 48] for i in range(4)]).astype(BF)


def turn_rows():
    turn = np.zeros((RT * U, RT * U), np.float32)
    for z in range(RT):
        for u in range(U):
            turn[z * U + u, u * RT + z] = 1.0
    return jnp.asarray(turn, BF)


def tiles_kernel(values, rows, turn, out, wide):
    for g in range(G):
        for q in range(U // 4):
            wide[g * U : (g + 1) * U, q * 128 : (q + 1) * 128] = jnp.concatenate(
                [values[g, 4 * q + i].astype(F32) for i in range(4)], axis=1
            )
    flat = wide[...]
    blank = jnp.zeros((64, COLS), F32)
    even = jnp.concatenate([flat, blank], axis=0).astype(BF)
    odd = jnp.concatenate([blank, flat], axis=0).astype(BF)
    for q in range(4):
        turned = lax.dot_general(
            turn[q * ROWS : (q + 1) * ROWS, :],
            odd if q % 2 else even,
            (((1,), (1,)), ((), ())),
            preferred_element_type=F32,
        )
        if q % 2 == 0:
            kept = turned
        else:
            first = (q - 1) * ROWS
            out[:ROWS, first : first + 128] = kept[:, :128].astype(BF)
            out[:ROWS, first + 128 : first + 256] = (kept[:, 128:] + turned[:, :128]).astype(BF)
            out[:ROWS, first + 256 : first + 384] = turned[:, 128:].astype(BF)
    tile_rows = rows[...].astype(F32)
    line = [
        jnp.concatenate([tile_rows[4 * k + i : 4 * k + i + 1] for i in range(4)], axis=1)
        for k in range(2)
    ]
    line = jnp.concatenate(line + [jnp.zeros((1, COLS - G * RT), F32)], axis=1)
    out[ROWS:, :] = jnp.broadcast_to(line, (8, COLS)).astype(BF)


def stack_kernel(after, *refs):
    parts, out, sems = refs[:NZ], refs[NZ], refs[NZ + 1]
    copies = [pltpu.make_async_copy(parts[i], out.at[i], sems.at[i]) for i in range(NZ)]
    for cp in copies:
        cp.start()
    for cp in copies:
        cp.wait()


def add_products(labels, place, ps, xs, acc, pbuf, xbuf, spots_v, lists, psem, xsem, lsem, fresh):
    first_label, last_label = labels
    count = last_label - first_label
    pc, xc = [], []
    for i in range(count):
        k, side = (first_label + i) // 2, (first_label + i) % 2
        pc.append(pltpu.make_async_copy(ps[side].at[k], pbuf.at[i], psem.at[i]))
        xc.append(pltpu.make_async_copy(xs[i].at[side], xbuf.at[i], xsem.at[i]))
    for cp in pc + xc:
        cp.start()
    if fresh:
        acc[...] = jnp.zeros_like(acc)
    for cp in pc:
        cp.wait()
    for i in range(count):
        tile = pbuf[i, ROWS:, : G * RT].astype(F32)[0:1].astype(jnp.int32)
        to_y = ((tile >> 3) - place[0]) & (NY - 1)
        spots_v[i : i + 1] = (to_y * (G * NH) + (tile >> 5) * NH + (tile & 7)) * U
    to_smem = pltpu.make_async_copy(spots_v, lists, lsem)
    to_smem.start()
    for cp in xc:
        cp.wait()
    to_smem.wait()
    rows = lax.broadcasted_iota(jnp.int32, (ROWS, 128), 0)
    blank = jnp.zeros((64, 256), F32)

    @pl.loop(0, count)
    def _(label):
        x = jnp.concatenate(unpack(xbuf[label].astype(F32)), axis=0)
        for pair in range(4):
            sides = []
            for g in (2 * pair, 2 * pair + 1):
                keep = (rows >= g * U) & (rows < (g + 1) * U)
                sides.append(jnp.where(keep, x, 0.0))
            diag = jnp.concatenate(sides, axis=1)
            for odd in range(2):
                order = [blank, diag] if odd else [diag, blank]
                windows = []
                for q in (odd, odd + 2):
                    first = q * ROWS - odd * 64
                    windows.append(pbuf[label, :ROWS, first : first + 256])
                terms = jnp.dot(
                    jnp.concatenate(windows, axis=0),
                    jnp.concatenate(order, axis=0).astype(BF),
                    preferred_element_type=F32,
                )
                for side in range(2):
                    g = 2 * pair + side
                    for half in range(2):
                        spots, sums = [], []
                        for z in range(8):
                            row = lists[label, g * RT + (odd + 2 * half) * 8 + z]
                            spot = pl.ds(pl.multiple_of(row, 8), U)
                            spots.append(spot)
                            at = (half * 8 + z) * U
                            sums.append(
                                acc[spot, :] + terms[at : at + U, side * 128 : (side + 1) * 128]
                            )
                        for spot, total in zip(spots, sums):
                            acc[spot, :] = total


def finish_products(acc, own_ref, sends):
    size = ROWS * NH
    own_ref[...] = acc[0:size]
    quarter = size // 4
    for k, ref in enumerate(sends):
        first = (k + 1) * size
        ref[...] = pack(
            [acc[first + i * quarter : first + (i + 1) * quarter] for i in range(4)]
        ).astype(BF)


def first_kernel(place, *refs):
    ps, xs, acc, done = refs[:2], refs[2 : 2 + FIRST], refs[2 + FIRST], refs[3 + FIRST]
    add_products((0, FIRST), place, ps, xs, acc, *refs[4 + FIRST :], fresh=True)
    done[...] = jnp.zeros_like(done)


def last_kernel(place, *refs):
    more = NH - FIRST
    ps, xs = refs[:2], refs[2 : 2 + more]
    acc, own_ref, *sends = refs[4 + more : 9 + more]
    add_products((FIRST, NH), place, ps, xs, acc, *refs[9 + more :], fresh=False)
    finish_products(acc, own_ref, sends)


def a_kernel(place, *refs):
    ps, xs, (own_ref, *sends) = refs[:2], refs[2:10], refs[10:14]
    add_products((0, NH), place, ps, xs, *refs[14:], fresh=True)
    finish_products(refs[14], own_ref, sends)


def product_scratch(count):
    return [
        pltpu.VMEM((count, ROWS + 8, COLS), BF),
        pltpu.VMEM((count, ROWS // 4, 384), BF),
        pltpu.VMEM((count, G * RT), jnp.int32),
        pltpu.SMEM((count, G * RT), jnp.int32),
        pltpu.SemaphoreType.DMA((count,)),
        pltpu.SemaphoreType.DMA((count,)),
        pltpu.SemaphoreType.DMA,
    ]


def pair_kernel(stay, came, *refs):
    outs, sems = refs[:NZ], refs[NZ]
    copies = []
    for k in range(NZ):
        copies.append(pltpu.make_async_copy(stay.at[k], outs[k].at[0], sems.at[2 * k]))
        copies.append(pltpu.make_async_copy(came.at[k], outs[k].at[1], sems.at[2 * k + 1]))
    for cp in copies:
        cp.start()
    for cp in copies:
        cp.wait()


def y_kernel(dests, r2, own, r1, r3, ident, *refs):
    ds, m_ref, y = refs[:NC], refs[NC], refs[NC + 1]
    quarter = ROWS * NH // 4
    parts = [unpack(r[...].astype(F32)) for r in (r1, r2, r3)]
    for i in range(4):
        span = slice(i * quarter, (i + 1) * quarter)
        y[span, :] = own[span, :] + parts[0][i] + parts[1][i] + parts[2][i]
    for label in range(NH):
        h = dests[label]
        pieces = []
        for g in range(G):
            pieces.append(y[pl.ds(pl.multiple_of((g * NH + h) * U, 8), U), :])
        pairs = [jnp.concatenate(pieces[2 * i : 2 * i + 2], axis=0) for i in range(4)]
        ds[label % 2][label // 2] = pack(pairs).astype(BF)
    for g in range(G):
        block = y[g * ROWS : (g + 1) * ROWS, :].astype(BF)
        turned = lax.dot_general(
            ident[...], block, (((1,), (1,)), ((), ())), preferred_element_type=F32
        )
        for ys in range(NY):
            m_ref[ys * G + g] = turned[ys * U : (ys + 1) * U, :].astype(BF)


def out_kernel(*refs):
    ds, (m_ref, perm_ref, gaps, out_ref) = refs[1:NZ] + refs[:1], refs[NZ:]
    total = jnp.zeros((ROWS, COLS), F32)
    for label in range(NH):
        packed = ds[label // 2][label % 2].astype(F32)
        piece = jnp.concatenate(unpack(packed), axis=0).astype(BF)
        total = total + jnp.dot(piece, perm_ref[label], preferred_element_type=F32)
    row = lax.broadcasted_iota(jnp.int32, (ROWS, COLS), 0)
    col = lax.broadcasted_iota(jnp.int32, (ROWS, COLS), 1)
    for ys in range(NY):
        place = jnp.where(col == row + ys * ROWS, 1.0, 0.0).astype(BF)
        total = total + jnp.dot(m_ref[ys], place, preferred_element_type=F32)
    out_ref[...] = total / gaps[...]


def cost(us):
    return pl.CostEstimate(flops=int(us * 1.15e9), bytes_accessed=1 << 20, transcendentals=0)


def params(mib):
    return pltpu.CompilerParams(vmem_limit_bytes=mib * 1024 * 1024)


def per_device(c_matrix, beta_values, beta_rows, alpha_values, alpha_rows, gaps):
    y, zh, core = lax.axis_index("y"), lax.axis_index("zh"), lax.axis_index("core")
    zl, x = lax.axis_index("zl"), lax.axis_index("x")
    sign = 1 - 2 * zl
    steps = jnp.array([s for s in STEPS for _ in range(NC)], jnp.int32)
    flips = jnp.array([0, 1] * NZ, jnp.int32)
    h_to = (zh + sign * steps) % NZ * NC + (core ^ flips)
    h_from = (zh - sign * steps) % NZ * NC + (core ^ flips)

    c_own = c_matrix.reshape(ROWS, COLS)
    over, left, right = flip_zl(c_own), shift_x(c_own, 1), shift_x(c_own, -1)
    over_right, far, over_left = shift_x(over, -1), shift_x(left, 1), shift_x(over, 1)
    over_far = shift_x(over_right, -1)
    blocks = [pltpu.with_memory_space_constraint(c_own, pltpu.HBM), right, far, left, over, over_right, over_far, over_left]

    tiles = pl.pallas_call(
        tiles_kernel,
        out_shape=jax.ShapeDtypeStruct((ROWS + 8, COLS), BF),
        in_specs=[VM] * 3,
        out_specs=VM,
        scratch_shapes=[pltpu.VMEM((ROWS, COLS), F32)],
        compiler_params=params(12),
        name="arrange_tiles",
    )(jnp.transpose(alpha_values[0, :, 0], (0, 2, 3, 1)), alpha_rows[0, :, 0], turn_rows())
    a_next = send_step(tiles, 2)
    a_near = [tiles, cross_z(tiles, 1), a_next, cross_z(a_next, 1)]

    col_block = beta_rows[0] // 6
    slots = (((col_block // NX) ^ zl) * NX + (col_block % NX - x) % NX) * 6 + beta_rows[0] % 6
    lane = jnp.arange(128, dtype=jnp.int32)
    place = jnp.where(lane < PART, lane // U * (NH * U) + lane % U, -COLS)
    cols = jnp.arange(COLS, dtype=jnp.int32)
    spread_to = (place[None, :] + h_to[:, None] * U).reshape(-1)
    perm_to = (cols[:, None] == spread_to[None, :]).astype(BF)
    perm_from = (cols[None, None, :] == (place[None, :] + h_from[:, None] * U)[:, :, None]).astype(BF)
    piece = jax.ShapeDtypeStruct((NC, ROWS // 4, 384), BF)
    x_out = pl.pallas_call(
        x_kernel,
        out_shape=[piece] * NZ,
        in_specs=[SM] + [VM] * 7 + [HBM] + [VM] * 2,
        out_specs=[VM] * NZ,
        scratch_shapes=[
            pltpu.VMEM((8, ROWS, COLS), BF),
            pltpu.VMEM((ROWS, COLS), BF),
            pltpu.SemaphoreType.DMA((8,)),
        ],
        compiler_params=params(12),
        name="beta_product",
    )(slots.reshape(-1), *[blocks[k] for k in ARRIVAL], beta_values[0].reshape(6, 768, 128), perm_to)
    direct = [x_out[0]] + [send_step(x_out[k], k) for k in range(1, NZ)]
    x_parts = direct + [flip_core(a) for a in direct[:3]]
    a_own = pl.pallas_call(
        stack_kernel,
        out_shape=jax.ShapeDtypeStruct((NZ, ROWS + 8, COLS), BF),
        in_specs=[HBM] * 5,
        out_specs=HBM,
        scratch_shapes=[pltpu.SemaphoreType.DMA((NZ,))],
        compiler_params=params(4),
        name="stack_tiles",
    )(x_out[0], *a_near)

    size = ROWS * NH
    part = jax.ShapeDtypeStruct((size // 4, 384), BF)
    by_label = [x_parts[i % 2 * NZ + i // 2] for i in range(FIRST)]
    a_pair = (a_own, flip_core(a_own))
    total = jax.ShapeDtypeStruct((size * NY, 128), F32)
    acc, done = pl.pallas_call(
        first_kernel,
        out_shape=[total, jax.ShapeDtypeStruct((8, 128), F32)],
        in_specs=[SM] + [HBM] * (2 + FIRST),
        out_specs=[VM] * 2,
        scratch_shapes=product_scratch(FIRST),
        compiler_params=params(16),
        cost_estimate=cost(6),
        name="alpha_product_first",
    )(y.reshape(1), *a_pair, *by_label)
    farthest, done = lax.optimization_barrier((direct[3], done))
    _, own, s1, s2, s3 = pl.pallas_call(
        last_kernel,
        out_shape=[total, jax.ShapeDtypeStruct((size, 128), F32), part, part, part],
        in_specs=[SM] + [HBM] * (2 + NH - FIRST) + [VM] * 2,
        out_specs=[VM] * 5,
        input_output_aliases={3 + NH - FIRST: 0},
        scratch_shapes=product_scratch(NH - FIRST),
        compiler_params=params(16),
        name="alpha_product_last",
    )(y.reshape(1), *a_pair, farthest, flip_core(farthest), acc, done)
    r2, r1, r3 = shift_y(s2, 2), shift_y(s1, 1), shift_y(s3, 3)

    y_out = pl.pallas_call(
        y_kernel,
        out_shape=[jax.ShapeDtypeStruct((NZ, ROWS // 4, 384), BF)] * NC
        + [jax.ShapeDtypeStruct((NY * G, U, ROWS), BF)],
        in_specs=[SM] + [VM] * 5,
        out_specs=[VM] * (NC + 1),
        scratch_shapes=[pltpu.VMEM((size, 128), F32)],
        compiler_params=params(12),
        name="y_sum",
    )(h_to, r2, own, r1, r3, jnp.eye(128, dtype=BF))
    came = flip_core(y_out[1])
    mirrored = lax.all_to_all(y_out[NC], ("y", "zl", "x"), split_axis=0, concat_axis=0, tiled=True)
    pairs = pl.pallas_call(
        pair_kernel,
        out_shape=[piece] * NZ,
        in_specs=[HBM] * 2,
        out_specs=[HBM] * NZ,
        scratch_shapes=[pltpu.SemaphoreType.DMA((2 * NZ,))],
        compiler_params=params(4),
        name="pair_pieces",
    )(y_out[0], came)
    d_parts = [pairs[0]] + [send_step(pairs[k], k) for k in range(1, NZ)]
    out = pl.pallas_call(
        out_kernel,
        out_shape=jax.ShapeDtypeStruct((ROWS, COLS), F32),
        in_specs=[VM] * (NZ + 3),
        out_specs=VM,
        compiler_params=params(12),
        name="combine",
    )(d_parts[3], *d_parts[:3], mirrored.reshape(NY, ROWS, ROWS), perm_from, gaps.reshape(ROWS, COLS))
    return out.reshape(gaps.shape)


def solution(mesh):
    fine = Mesh(mesh.devices.reshape(NY, NZ, NC, NL, NX), ("y", "zh", "core", "zl", "x"))
    row, col = ("y", "zh", "core"), ("zl", "x")
    placed = (
        P(None, row, col),
        P(None, col, None, None, None),
        P(None, col, None),
        P(None, None, row, None, None, None),
        P(None, None, row, None),
        P(None, row, col),
    )
    return jax.shard_map(
        per_device, mesh=fine, in_specs=placed, out_specs=P(None, row, col), check_vma=False
    )
```

```python
import jax
import jax.numpy as jnp
import numpy as np
from jax import lax
from jax.experimental import pallas as pl
from jax.experimental.pallas import tpu as pltpu
from jax.sharding import Mesh, PartitionSpec as P

BF = jnp.bfloat16
F32 = jnp.float32
NY, NZ, NC, NL, NX = 4, 4, 2, 2, 4
NH = NZ * NC
G, U, RT = 8, 24, 32
ROWS = G * U
COLS = 768
PART = COLS // NH
FIRST = 6
ARRIVAL = (4, 6, 5, 7, 3, 2, 1, 0)
STEPS = (0, 1, -1, 2)
HBM = pl.BlockSpec(memory_space=pltpu.HBM)
VM = pl.BlockSpec(memory_space=pltpu.VMEM)
SM = pl.BlockSpec(memory_space=pltpu.SMEM)


def shift_x(a, k):
    return lax.ppermute(a, "x", [(i, (i + k) % NX) for i in range(NX)])


def flip_zl(a):
    return lax.ppermute(a, "zl", [(0, 1), (1, 0)])


def flip_core(a):
    return lax.ppermute(a, "core", [(0, 1), (1, 0)])


def shift_y(a, k):
    return lax.ppermute(a, "y", [(i, (i + k) % NY) for i in range(NY)])


def cross_z(a, step):
    moves = []
    for zh in range(NZ):
        moves.append((zh * 2, (zh - step) % NZ * 2 + 1))
        moves.append((zh * 2 + 1, (zh + step) % NZ * 2))
    return lax.ppermute(a, ("zh", "zl"), moves)


def send_step(a, label):
    moves = []
    for zh in range(NZ):
        for zl in range(NL):
            to = (zh + (1 - 2 * zl) * STEPS[label]) % NZ
            moves.append((zh * 2 + zl, to * 2 + zl))
    return lax.ppermute(a, ("zh", "zl"), moves)


def pack(pieces):
    lane = lax.broadcasted_iota(jnp.int32, pieces[0].shape, 1)
    p0, r1, r2, r3 = pieces[0], *(pltpu.roll(pieces[i], 128 - 32 * i, 1) for i in (1, 2, 3))
    return jnp.concatenate(
        [
            jnp.where(lane < 96, p0, r1),
            jnp.where(lane < 64, r1, r2),
            jnp.where(lane < 32, r2, r3),
        ],
        axis=1,
    )


def unpack(packed):
    t0, t1, t2 = (packed[:, i * 128 : (i + 1) * 128] for i in range(3))
    lane = lax.broadcasted_iota(jnp.int32, t0.shape, 1)
    return [
        t0,
        pltpu.roll(jnp.where(lane < 96, t1, t0), 32, 1),
        pltpu.roll(jnp.where(lane < 64, t2, t1), 64, 1),
        pltpu.roll(t2, 96, 1),
    ]


def x_kernel(slots, *refs):
    blocks, (b_ref, perm_ref), outs = refs[:8], refs[8:10], refs[10 : 10 + NZ]
    cbuf, xs, sems = refs[10 + NZ :]
    copies = [pltpu.make_async_copy(blocks[i], cbuf.at[k], sems.at[i]) for i, k in enumerate(ARRIVAL)]
    for cp in copies:
        cp.start()
    for cp in copies:
        cp.wait()
    for j in range(6):
        picked = []
        for z in range(6):
            slot = slots[j * 6 + z]
            k, t = slot // 6, slot % 6
            picked.append(cbuf[k, :, pl.ds(pl.multiple_of(t * 128, 128), 128)])
        lhs = jnp.concatenate(picked, axis=1)
        xs[:, j * 128 : (j + 1) * 128] = jnp.dot(
            lhs, b_ref[j], preferred_element_type=F32
        ).astype(BF)
    for label in range(NH):
        piece = jnp.dot(
            xs[...], perm_ref[:, label * 128 : (label + 1) * 128], preferred_element_type=F32
        )
        outs[label // 2][label % 2] = pack([piece[i * 48 : (i + 1) * 48] for i in range(4)]).astype(BF)


def turn_rows():
    turn = np.zeros((RT * U, RT * U), np.float32)
    for z in range(RT):
        for u in range(U):
            turn[z * U + u, u * RT + z] = 1.0
    return jnp.asarray(turn, BF)


def tiles_kernel(values, rows, turn, out, wide):
    for g in range(G):
        for q in range(U // 4):
            wide[g * U : (g + 1) * U, q * 128 : (q + 1) * 128] = jnp.concatenate(
                [values[g, 4 * q + i].astype(F32) for i in range(4)], axis=1
            )
    flat = wide[...]
    blank = jnp.zeros((64, COLS), F32)
    even = jnp.concatenate([flat, blank], axis=0).astype(BF)
    odd = jnp.concatenate([blank, flat], axis=0).astype(BF)
    for q in range(4):
        turned = lax.dot_general(
            turn[q * ROWS : (q + 1) * ROWS, :],
            odd if q % 2 else even,
            (((1,), (1,)), ((), ())),
            preferred_element_type=F32,
        )
        if q % 2 == 0:
            kept = turned
        else:
            first = (q - 1) * ROWS
            out[:ROWS, first : first + 128] = kept[:, :128].astype(BF)
            out[:ROWS, first + 128 : first + 256] = (kept[:, 128:] + turned[:, :128]).astype(BF)
            out[:ROWS, first + 256 : first + 384] = turned[:, 128:].astype(BF)
    tile_rows = rows[...].astype(F32)
    line = [
        jnp.concatenate([tile_rows[4 * k + i : 4 * k + i + 1] for i in range(4)], axis=1)
        for k in range(2)
    ]
    line = jnp.concatenate(line + [jnp.zeros((1, COLS - G * RT), F32)], axis=1)
    out[ROWS:, :] = jnp.broadcast_to(line, (8, COLS)).astype(BF)


def stack_kernel(after, *refs):
    count = NZ - 1
    parts, out, sems = refs[:count], refs[count], refs[count + 1]
    copies = [pltpu.make_async_copy(parts[i], out.at[i], sems.at[i]) for i in range(count)]
    for cp in copies:
        cp.start()
    for cp in copies:
        cp.wait()


def add_products(labels, place, ps, xs, acc, pbuf, xbuf, spots_v, lists, psem, xsem, lsem, fresh):
    first_label, last_label = labels
    count = last_label - first_label
    pc, xc = [], []
    for i in range(count):
        k, side = (first_label + i) // 2, (first_label + i) % 2
        tiles = ps[side].at[k] if fresh else ps[side]
        pc.append(pltpu.make_async_copy(tiles, pbuf.at[i], psem.at[i]))
        xc.append(pltpu.make_async_copy(xs[i].at[side], xbuf.at[i], xsem.at[i]))
    for cp in pc + xc:
        cp.start()
    if fresh:
        acc[...] = jnp.zeros_like(acc)
    for cp in pc:
        cp.wait()
    for i in range(count):
        tile = pbuf[i, ROWS:, : G * RT].astype(F32)[0:1].astype(jnp.int32)
        to_y = ((tile >> 3) - place[0]) & (NY - 1)
        spots_v[i : i + 1] = (to_y * (G * NH) + (tile >> 5) * NH + (tile & 7)) * U
    to_smem = pltpu.make_async_copy(spots_v, lists, lsem)
    to_smem.start()
    for cp in xc:
        cp.wait()
    to_smem.wait()
    rows = lax.broadcasted_iota(jnp.int32, (ROWS, 128), 0)
    blank = jnp.zeros((64, 256), F32)

    @pl.loop(0, count)
    def _(label):
        x = jnp.concatenate(unpack(xbuf[label].astype(F32)), axis=0)
        for pair in range(4):
            sides = []
            for g in (2 * pair, 2 * pair + 1):
                keep = (rows >= g * U) & (rows < (g + 1) * U)
                sides.append(jnp.where(keep, x, 0.0))
            diag = jnp.concatenate(sides, axis=1)
            for odd in range(2):
                order = [blank, diag] if odd else [diag, blank]
                windows = []
                for q in (odd, odd + 2):
                    first = q * ROWS - odd * 64
                    windows.append(pbuf[label, :ROWS, first : first + 256])
                terms = jnp.dot(
                    jnp.concatenate(windows, axis=0),
                    jnp.concatenate(order, axis=0).astype(BF),
                    preferred_element_type=F32,
                )
                for side in range(2):
                    g = 2 * pair + side
                    for half in range(2):
                        spots, sums = [], []
                        for z in range(8):
                            row = lists[label, g * RT + (odd + 2 * half) * 8 + z]
                            spot = pl.ds(pl.multiple_of(row, 8), U)
                            spots.append(spot)
                            at = (half * 8 + z) * U
                            sums.append(
                                acc[spot, :] + terms[at : at + U, side * 128 : (side + 1) * 128]
                            )
                        for spot, total in zip(spots, sums):
                            acc[spot, :] = total


def finish_products(acc, own_ref, sends):
    size = ROWS * NH
    own_ref[...] = acc[0:size]
    quarter = size // 4
    for k, ref in enumerate(sends):
        first = (k + 1) * size
        ref[...] = pack(
            [acc[first + i * quarter : first + (i + 1) * quarter] for i in range(4)]
        ).astype(BF)


def first_kernel(place, *refs):
    ps, xs, acc, done = refs[:2], refs[2 : 2 + FIRST], refs[2 + FIRST], refs[3 + FIRST]
    add_products((0, FIRST), place, ps, xs, acc, *refs[4 + FIRST :], fresh=True)
    done[...] = jnp.zeros_like(done)


def last_kernel(place, *refs):
    more = NH - FIRST
    ps, xs = refs[:2], refs[2 : 2 + more]
    acc, own_ref, *sends = refs[4 + more : 9 + more]
    add_products((FIRST, NH), place, ps, xs, acc, *refs[9 + more :], fresh=False)
    finish_products(acc, own_ref, sends)


def product_scratch(count):
    return [
        pltpu.VMEM((count, ROWS + 8, COLS), BF),
        pltpu.VMEM((count, ROWS // 4, 384), BF),
        pltpu.VMEM((count, G * RT), jnp.int32),
        pltpu.SMEM((count, G * RT), jnp.int32),
        pltpu.SemaphoreType.DMA((count,)),
        pltpu.SemaphoreType.DMA((count,)),
        pltpu.SemaphoreType.DMA,
    ]


def pair_kernel(stay, came, *refs):
    outs, sems = refs[:NZ], refs[NZ]
    copies = []
    for k in range(NZ):
        copies.append(pltpu.make_async_copy(stay.at[k], outs[k].at[0], sems.at[2 * k]))
        copies.append(pltpu.make_async_copy(came.at[k], outs[k].at[1], sems.at[2 * k + 1]))
    for cp in copies:
        cp.start()
    for cp in copies:
        cp.wait()


def y_kernel(dests, r2, own, r1, r3, ident, *refs):
    ds, m_ref, y = refs[:NC], refs[NC], refs[NC + 1]
    quarter = ROWS * NH // 4
    parts = [unpack(r[...].astype(F32)) for r in (r1, r2, r3)]
    for i in range(4):
        span = slice(i * quarter, (i + 1) * quarter)
        y[span, :] = own[span, :] + parts[0][i] + parts[1][i] + parts[2][i]
    for label in range(NH):
        h = dests[label]
        pieces = []
        for g in range(G):
            pieces.append(y[pl.ds(pl.multiple_of((g * NH + h) * U, 8), U), :])
        pairs = [jnp.concatenate(pieces[2 * i : 2 * i + 2], axis=0) for i in range(4)]
        ds[label % 2][label // 2] = pack(pairs).astype(BF)
    for g in range(G):
        block = y[g * ROWS : (g + 1) * ROWS, :].astype(BF)
        turned = lax.dot_general(
            ident[...], block, (((1,), (1,)), ((), ())), preferred_element_type=F32
        )
        for ys in range(NY):
            m_ref[ys * G + g] = turned[ys * U : (ys + 1) * U, :].astype(BF)


def out_kernel(*refs):
    ds, (m_ref, perm_ref, gaps, out_ref) = refs[1:NZ] + refs[:1], refs[NZ:]
    total = jnp.zeros((ROWS, COLS), F32)
    for label in range(NH):
        packed = ds[label // 2][label % 2].astype(F32)
        piece = jnp.concatenate(unpack(packed), axis=0).astype(BF)
        total = total + jnp.dot(piece, perm_ref[label], preferred_element_type=F32)
    row = lax.broadcasted_iota(jnp.int32, (ROWS, COLS), 0)
    col = lax.broadcasted_iota(jnp.int32, (ROWS, COLS), 1)
    for ys in range(NY):
        place = jnp.where(col == row + ys * ROWS, 1.0, 0.0).astype(BF)
        total = total + jnp.dot(m_ref[ys], place, preferred_element_type=F32)
    out_ref[...] = total / gaps[...]


def cost(us):
    return pl.CostEstimate(flops=int(us * 1.15e9), bytes_accessed=1 << 20, transcendentals=0)


def params(mib):
    return pltpu.CompilerParams(vmem_limit_bytes=mib * 1024 * 1024)


def per_device(c_matrix, beta_values, beta_rows, alpha_values, alpha_rows, gaps):
    y, zh, core = lax.axis_index("y"), lax.axis_index("zh"), lax.axis_index("core")
    zl, x = lax.axis_index("zl"), lax.axis_index("x")
    sign = 1 - 2 * zl
    steps = jnp.array([s for s in STEPS for _ in range(NC)], jnp.int32)
    flips = jnp.array([0, 1] * NZ, jnp.int32)
    h_to = (zh + sign * steps) % NZ * NC + (core ^ flips)
    h_from = (zh - sign * steps) % NZ * NC + (core ^ flips)

    c_own = c_matrix.reshape(ROWS, COLS)
    over, left, right = flip_zl(c_own), shift_x(c_own, 1), shift_x(c_own, -1)
    over_right, far, over_left = shift_x(over, -1), shift_x(left, 1), shift_x(over, 1)
    over_far = shift_x(over_right, -1)
    blocks = [pltpu.with_memory_space_constraint(c_own, pltpu.HBM), right, far, left, over, over_right, over_far, over_left]

    tiles = pl.pallas_call(
        tiles_kernel,
        out_shape=jax.ShapeDtypeStruct((ROWS + 8, COLS), BF),
        in_specs=[VM] * 3,
        out_specs=VM,
        scratch_shapes=[pltpu.VMEM((ROWS, COLS), F32)],
        compiler_params=params(12),
        name="arrange_tiles",
    )(jnp.transpose(alpha_values[0, :, 0], (0, 2, 3, 1)), alpha_rows[0, :, 0], turn_rows())
    a_near = [tiles, cross_z(tiles, 1), send_step(tiles, 2)]
    a_far = cross_z(tiles, 2)

    col_block = beta_rows[0] // 6
    slots = (((col_block // NX) ^ zl) * NX + (col_block % NX - x) % NX) * 6 + beta_rows[0] % 6
    lane = jnp.arange(128, dtype=jnp.int32)
    place = jnp.where(lane < PART, lane // U * (NH * U) + lane % U, -COLS)
    cols = jnp.arange(COLS, dtype=jnp.int32)
    spread_to = (place[None, :] + h_to[:, None] * U).reshape(-1)
    perm_to = (cols[:, None] == spread_to[None, :]).astype(BF)
    perm_from = (cols[None, None, :] == (place[None, :] + h_from[:, None] * U)[:, :, None]).astype(BF)
    piece = jax.ShapeDtypeStruct((NC, ROWS // 4, 384), BF)
    x_out = pl.pallas_call(
        x_kernel,
        out_shape=[piece] * NZ,
        in_specs=[SM] + [VM] * 7 + [HBM] + [VM] * 2,
        out_specs=[VM] * NZ,
        scratch_shapes=[
            pltpu.VMEM((8, ROWS, COLS), BF),
            pltpu.VMEM((ROWS, COLS), BF),
            pltpu.SemaphoreType.DMA((8,)),
        ],
        compiler_params=params(12),
        name="beta_product",
    )(slots.reshape(-1), *[blocks[k] for k in ARRIVAL], beta_values[0].reshape(6, 768, 128), perm_to)
    direct = [x_out[0]] + [send_step(x_out[k], k) for k in range(1, NZ)]
    x_parts = direct + [flip_core(a) for a in direct[:3]]
    a_own = pl.pallas_call(
        stack_kernel,
        out_shape=jax.ShapeDtypeStruct((NZ - 1, ROWS + 8, COLS), BF),
        in_specs=[HBM] * NZ,
        out_specs=HBM,
        scratch_shapes=[pltpu.SemaphoreType.DMA((NZ - 1,))],
        compiler_params=params(4),
        name="stack_tiles",
    )(x_out[0], *a_near)

    size = ROWS * NH
    part = jax.ShapeDtypeStruct((size // 4, 384), BF)
    by_label = [x_parts[i % 2 * NZ + i // 2] for i in range(FIRST)]
    a_pair = (a_own, flip_core(a_own))
    total = jax.ShapeDtypeStruct((size * NY, 128), F32)
    acc, done = pl.pallas_call(
        first_kernel,
        out_shape=[total, jax.ShapeDtypeStruct((8, 128), F32)],
        in_specs=[SM] + [HBM] * (2 + FIRST),
        out_specs=[VM] * 2,
        scratch_shapes=product_scratch(FIRST),
        compiler_params=params(16),
        cost_estimate=cost(6),
        name="alpha_product_first",
    )(y.reshape(1), *a_pair, *by_label)
    farthest, a_far, done = lax.optimization_barrier((direct[3], a_far, done))
    _, own, s1, s2, s3 = pl.pallas_call(
        last_kernel,
        out_shape=[total, jax.ShapeDtypeStruct((size, 128), F32), part, part, part],
        in_specs=[SM] + [HBM] * (2 + NH - FIRST) + [VM] * 2,
        out_specs=[VM] * 5,
        input_output_aliases={3 + NH - FIRST: 0},
        scratch_shapes=product_scratch(NH - FIRST),
        compiler_params=params(16),
        name="alpha_product_last",
    )(y.reshape(1), a_far, flip_core(a_far), farthest, flip_core(farthest), acc, done)
    r2, r1, r3 = shift_y(s2, 2), shift_y(s1, 1), shift_y(s3, 3)

    y_out = pl.pallas_call(
        y_kernel,
        out_shape=[jax.ShapeDtypeStruct((NZ, ROWS // 4, 384), BF)] * NC
        + [jax.ShapeDtypeStruct((NY * G, U, ROWS), BF)],
        in_specs=[SM] + [VM] * 5,
        out_specs=[VM] * (NC + 1),
        scratch_shapes=[pltpu.VMEM((size, 128), F32)],
        compiler_params=params(12),
        name="y_sum",
    )(h_to, r2, own, r1, r3, jnp.eye(128, dtype=BF))
    came = flip_core(y_out[1])
    mirrored = lax.all_to_all(y_out[NC], ("y", "zl", "x"), split_axis=0, concat_axis=0, tiled=True)
    pairs = pl.pallas_call(
        pair_kernel,
        out_shape=[piece] * NZ,
        in_specs=[HBM] * 2,
        out_specs=[HBM] * NZ,
        scratch_shapes=[pltpu.SemaphoreType.DMA((2 * NZ,))],
        compiler_params=params(4),
        name="pair_pieces",
    )(y_out[0], came)
    d_parts = [pairs[0]] + [send_step(pairs[k], k) for k in range(1, NZ)]
    out = pl.pallas_call(
        out_kernel,
        out_shape=jax.ShapeDtypeStruct((ROWS, COLS), F32),
        in_specs=[VM] * (NZ + 3),
        out_specs=VM,
        compiler_params=params(12),
        name="combine",
    )(d_parts[3], *d_parts[:3], mirrored.reshape(NY, ROWS, ROWS), perm_from, gaps.reshape(ROWS, COLS))
    return out.reshape(gaps.shape)


def solution(mesh):
    fine = Mesh(mesh.devices.reshape(NY, NZ, NC, NL, NX), ("y", "zh", "core", "zl", "x"))
    row, col = ("y", "zh", "core"), ("zl", "x")
    placed = (
        P(None, row, col),
        P(None, col, None, None, None),
        P(None, col, None),
        P(None, None, row, None, None, None),
        P(None, None, row, None),
        P(None, row, col),
    )
    return jax.shard_map(
        per_device, mesh=fine, in_specs=placed, out_specs=P(None, row, col), check_vma=False
    )
```

```python
import jax
import jax.numpy as jnp
import numpy as np
from jax import lax
from jax.experimental import pallas as pl
from jax.experimental.pallas import tpu as pltpu
from jax.sharding import Mesh, PartitionSpec as P

BF = jnp.bfloat16
F32 = jnp.float32
NY, NZ, NC, NL, NX = 4, 4, 2, 2, 4
NH = NZ * NC
G, U, RT = 8, 24, 32
ROWS = G * U
COLS = 768
PART = COLS // NH
FIRST = 6
ARRIVAL = (4, 6, 5, 7, 3, 2, 1, 0)
STEPS = (0, 1, -1, 2)
HBM = pl.BlockSpec(memory_space=pltpu.HBM)
VM = pl.BlockSpec(memory_space=pltpu.VMEM)
SM = pl.BlockSpec(memory_space=pltpu.SMEM)


def shift_x(a, k):
    return lax.ppermute(a, "x", [(i, (i + k) % NX) for i in range(NX)])


def flip_zl(a):
    return lax.ppermute(a, "zl", [(0, 1), (1, 0)])


def flip_core(a):
    return lax.ppermute(a, "core", [(0, 1), (1, 0)])


def shift_y(a, k):
    return lax.ppermute(a, "y", [(i, (i + k) % NY) for i in range(NY)])


def cross_z(a, step):
    moves = []
    for zh in range(NZ):
        moves.append((zh * 2, (zh - step) % NZ * 2 + 1))
        moves.append((zh * 2 + 1, (zh + step) % NZ * 2))
    return lax.ppermute(a, ("zh", "zl"), moves)


def send_step(a, label):
    moves = []
    for zh in range(NZ):
        for zl in range(NL):
            to = (zh + (1 - 2 * zl) * STEPS[label]) % NZ
            moves.append((zh * 2 + zl, to * 2 + zl))
    return lax.ppermute(a, ("zh", "zl"), moves)


def pack(pieces):
    lane = lax.broadcasted_iota(jnp.int32, pieces[0].shape, 1)
    p0, r1, r2, r3 = pieces[0], *(pltpu.roll(pieces[i], 128 - 32 * i, 1) for i in (1, 2, 3))
    return jnp.concatenate(
        [
            jnp.where(lane < 96, p0, r1),
            jnp.where(lane < 64, r1, r2),
            jnp.where(lane < 32, r2, r3),
        ],
        axis=1,
    )


def unpack(packed):
    t0, t1, t2 = (packed[:, i * 128 : (i + 1) * 128] for i in range(3))
    lane = lax.broadcasted_iota(jnp.int32, t0.shape, 1)
    return [
        t0,
        pltpu.roll(jnp.where(lane < 96, t1, t0), 32, 1),
        pltpu.roll(jnp.where(lane < 64, t2, t1), 64, 1),
        pltpu.roll(t2, 96, 1),
    ]


def x_kernel(slots, *refs):
    blocks, (b_ref, perm_ref), outs = refs[:8], refs[8:10], refs[10 : 10 + NZ]
    cbuf, xs, sems = refs[10 + NZ :]
    copies = [pltpu.make_async_copy(blocks[i], cbuf.at[k], sems.at[i]) for i, k in enumerate(ARRIVAL)]
    for cp in copies:
        cp.start()
    for cp in copies:
        cp.wait()
    for j in range(6):
        picked = []
        for z in range(6):
            slot = slots[j * 6 + z]
            k, t = slot // 6, slot % 6
            picked.append(cbuf[k, :, pl.ds(pl.multiple_of(t * 128, 128), 128)])
        lhs = jnp.concatenate(picked, axis=1)
        xs[:, j * 128 : (j + 1) * 128] = jnp.dot(
            lhs, b_ref[j], preferred_element_type=F32
        ).astype(BF)
    for label in range(NH):
        piece = jnp.dot(
            xs[...], perm_ref[:, label * 128 : (label + 1) * 128], preferred_element_type=F32
        )
        outs[label // 2][label % 2] = pack([piece[i * 48 : (i + 1) * 48] for i in range(4)]).astype(BF)


def turn_rows():
    turn = np.zeros((RT * U, RT * U), np.float32)
    for z in range(RT):
        for u in range(U):
            turn[z * U + u, u * RT + z] = 1.0
    return jnp.asarray(turn, BF)


def tiles_kernel(values, rows, turn, out, wide):
    for g in range(G):
        for q in range(U // 4):
            wide[g * U : (g + 1) * U, q * 128 : (q + 1) * 128] = jnp.concatenate(
                [values[g, 4 * q + i].astype(F32) for i in range(4)], axis=1
            )
    flat = wide[...]
    blank = jnp.zeros((64, COLS), F32)
    even = jnp.concatenate([flat, blank], axis=0).astype(BF)
    odd = jnp.concatenate([blank, flat], axis=0).astype(BF)
    for q in range(4):
        turned = lax.dot_general(
            turn[q * ROWS : (q + 1) * ROWS, :],
            odd if q % 2 else even,
            (((1,), (1,)), ((), ())),
            preferred_element_type=F32,
        )
        if q % 2 == 0:
            kept = turned
        else:
            first = (q - 1) * ROWS
            out[:ROWS, first : first + 128] = kept[:, :128].astype(BF)
            out[:ROWS, first + 128 : first + 256] = (kept[:, 128:] + turned[:, :128]).astype(BF)
            out[:ROWS, first + 256 : first + 384] = turned[:, 128:].astype(BF)
    tile_rows = rows[...].astype(F32)
    line = [
        jnp.concatenate([tile_rows[4 * k + i : 4 * k + i + 1] for i in range(4)], axis=1)
        for k in range(2)
    ]
    line = jnp.concatenate(line + [jnp.zeros((1, COLS - G * RT), F32)], axis=1)
    out[ROWS:, :] = jnp.broadcast_to(line, (8, COLS)).astype(BF)


def stack_kernel(after, *refs):
    count = NZ - 1
    parts, out, sems = refs[:count], refs[count], refs[count + 1]
    copies = [pltpu.make_async_copy(parts[i], out.at[i], sems.at[i]) for i in range(count)]
    for cp in copies:
        cp.start()
    for cp in copies:
        cp.wait()


def add_products(labels, place, ps, xs, acc, pbuf, xbuf, spots_v, lists, psem, xsem, lsem, fresh):
    first_label, last_label = labels
    count = last_label - first_label
    pc, xc = [], []
    for i in range(count):
        k, side = (first_label + i) // 2, (first_label + i) % 2
        tiles = ps[side].at[k] if fresh else ps[side]
        pc.append(pltpu.make_async_copy(tiles, pbuf.at[i], psem.at[i]))
        xc.append(pltpu.make_async_copy(xs[i].at[side], xbuf.at[i], xsem.at[i]))
    for cp in pc + xc:
        cp.start()
    if fresh:
        acc[...] = jnp.zeros_like(acc)
    for cp in pc:
        cp.wait()
    for i in range(count):
        tile = pbuf[i, ROWS:, : G * RT].astype(F32)[0:1].astype(jnp.int32)
        to_y = ((tile >> 3) - place[0]) & (NY - 1)
        spots_v[i : i + 1] = (to_y * (G * NH) + (tile >> 5) * NH + (tile & 7)) * U
    to_smem = pltpu.make_async_copy(spots_v, lists, lsem)
    to_smem.start()
    for cp in xc:
        cp.wait()
    to_smem.wait()
    rows = lax.broadcasted_iota(jnp.int32, (ROWS, 128), 0)
    blank = jnp.zeros((64, 256), F32)

    @pl.loop(0, count)
    def _(label):
        x = jnp.concatenate(unpack(xbuf[label].astype(F32)), axis=0)
        for pair in range(4):
            sides = []
            for g in (2 * pair, 2 * pair + 1):
                keep = (rows >= g * U) & (rows < (g + 1) * U)
                sides.append(jnp.where(keep, x, 0.0))
            diag = jnp.concatenate(sides, axis=1)
            for odd in range(2):
                order = [blank, diag] if odd else [diag, blank]
                windows = []
                for q in (odd, odd + 2):
                    first = q * ROWS - odd * 64
                    windows.append(pbuf[label, :ROWS, first : first + 256])
                terms = jnp.dot(
                    jnp.concatenate(windows, axis=0),
                    jnp.concatenate(order, axis=0).astype(BF),
                    preferred_element_type=F32,
                )
                for side in range(2):
                    g = 2 * pair + side
                    for half in range(2):
                        spots, sums = [], []
                        for z in range(8):
                            row = lists[label, g * RT + (odd + 2 * half) * 8 + z]
                            spot = pl.ds(pl.multiple_of(row, 8), U)
                            spots.append(spot)
                            at = (half * 8 + z) * U
                            sums.append(
                                acc[spot, :] + terms[at : at + U, side * 128 : (side + 1) * 128]
                            )
                        for spot, total in zip(spots, sums):
                            acc[spot, :] = total


def finish_products(acc, own_ref, sends):
    size = ROWS * NH
    own_ref[...] = acc[0:size]
    quarter = size // 4
    for k, ref in enumerate(sends):
        first = (k + 1) * size
        ref[...] = pack(
            [acc[first + i * quarter : first + (i + 1) * quarter] for i in range(4)]
        ).astype(BF)


def first_kernel(place, *refs):
    ps, xs, acc, done = refs[:2], refs[2 : 2 + FIRST], refs[3 + FIRST], refs[4 + FIRST]
    add_products((0, FIRST), place, ps, xs, acc, *refs[5 + FIRST :], fresh=True)
    done[...] = jnp.zeros_like(done)


def last_kernel(place, *refs):
    more = NH - FIRST
    ps, xs = refs[:2], refs[2 : 2 + more]
    acc, own_ref, *sends = refs[4 + more : 9 + more]
    add_products((FIRST, NH), place, ps, xs, acc, *refs[9 + more :], fresh=False)
    finish_products(acc, own_ref, sends)


def product_scratch(count):
    return [
        pltpu.VMEM((count, ROWS + 8, COLS), BF),
        pltpu.VMEM((count, ROWS // 4, 384), BF),
        pltpu.VMEM((count, G * RT), jnp.int32),
        pltpu.SMEM((count, G * RT), jnp.int32),
        pltpu.SemaphoreType.DMA((count,)),
        pltpu.SemaphoreType.DMA((count,)),
        pltpu.SemaphoreType.DMA,
    ]


def pair_kernel(stay, came, *refs):
    outs, sems = refs[:NZ], refs[NZ]
    copies = []
    for k in range(NZ):
        copies.append(pltpu.make_async_copy(stay.at[k], outs[k].at[0], sems.at[2 * k]))
        copies.append(pltpu.make_async_copy(came.at[k], outs[k].at[1], sems.at[2 * k + 1]))
    for cp in copies:
        cp.start()
    for cp in copies:
        cp.wait()


def y_kernel(dests, r2, own, r1, r3, ident, *refs):
    ds, m_ref, y = refs[:NC], refs[NC], refs[NC + 1]
    quarter = ROWS * NH // 4
    parts = [unpack(r[...].astype(F32)) for r in (r1, r2, r3)]
    for i in range(4):
        span = slice(i * quarter, (i + 1) * quarter)
        y[span, :] = own[span, :] + parts[0][i] + parts[1][i] + parts[2][i]
    for label in range(NH):
        h = dests[label]
        pieces = []
        for g in range(G):
            pieces.append(y[pl.ds(pl.multiple_of((g * NH + h) * U, 8), U), :])
        pairs = [jnp.concatenate(pieces[2 * i : 2 * i + 2], axis=0) for i in range(4)]
        ds[label % 2][label // 2] = pack(pairs).astype(BF)
    for g in range(G):
        block = y[g * ROWS : (g + 1) * ROWS, :].astype(BF)
        turned = lax.dot_general(
            ident[...], block, (((1,), (1,)), ((), ())), preferred_element_type=F32
        )
        for ys in range(NY):
            m_ref[ys * G + g] = turned[ys * U : (ys + 1) * U, :].astype(BF)


def out_kernel(*refs):
    ds, (m_ref, perm_ref, gaps, out_ref) = refs[1:NZ] + refs[:1], refs[NZ:]
    total = jnp.zeros((ROWS, COLS), F32)
    for label in range(NH):
        packed = ds[label // 2][label % 2].astype(F32)
        piece = jnp.concatenate(unpack(packed), axis=0).astype(BF)
        total = total + jnp.dot(piece, perm_ref[label], preferred_element_type=F32)
    row = lax.broadcasted_iota(jnp.int32, (ROWS, COLS), 0)
    col = lax.broadcasted_iota(jnp.int32, (ROWS, COLS), 1)
    for ys in range(NY):
        place = jnp.where(col == row + ys * ROWS, 1.0, 0.0).astype(BF)
        total = total + jnp.dot(m_ref[ys], place, preferred_element_type=F32)
    out_ref[...] = total / gaps[...]


def cost(us):
    return pl.CostEstimate(flops=int(us * 1.15e9), bytes_accessed=1 << 20, transcendentals=0)


def params(mib):
    return pltpu.CompilerParams(vmem_limit_bytes=mib * 1024 * 1024)


def per_device(c_matrix, beta_values, beta_rows, alpha_values, alpha_rows, gaps):
    y, zh, core = lax.axis_index("y"), lax.axis_index("zh"), lax.axis_index("core")
    zl, x = lax.axis_index("zl"), lax.axis_index("x")
    sign = 1 - 2 * zl
    steps = jnp.array([s for s in STEPS for _ in range(NC)], jnp.int32)
    flips = jnp.array([0, 1] * NZ, jnp.int32)
    h_to = (zh + sign * steps) % NZ * NC + (core ^ flips)
    h_from = (zh - sign * steps) % NZ * NC + (core ^ flips)

    c_own = c_matrix.reshape(ROWS, COLS)
    over, left, right = flip_zl(c_own), shift_x(c_own, 1), shift_x(c_own, -1)
    over_right, far, over_left = shift_x(over, -1), shift_x(left, 1), shift_x(over, 1)
    over_far = shift_x(over_right, -1)
    blocks = [pltpu.with_memory_space_constraint(c_own, pltpu.HBM), right, far, left, over, over_right, over_far, over_left]

    tiles = pl.pallas_call(
        tiles_kernel,
        out_shape=jax.ShapeDtypeStruct((ROWS + 8, COLS), BF),
        in_specs=[VM] * 3,
        out_specs=VM,
        scratch_shapes=[pltpu.VMEM((ROWS, COLS), F32)],
        compiler_params=params(12),
        name="arrange_tiles",
    )(jnp.transpose(alpha_values[0, :, 0], (0, 2, 3, 1)), alpha_rows[0, :, 0], turn_rows())
    a_near = [tiles, cross_z(tiles, 1), send_step(tiles, 2)]
    a_far = cross_z(tiles, 2)

    col_block = beta_rows[0] // 6
    slots = (((col_block // NX) ^ zl) * NX + (col_block % NX - x) % NX) * 6 + beta_rows[0] % 6
    lane = jnp.arange(128, dtype=jnp.int32)
    place = jnp.where(lane < PART, lane // U * (NH * U) + lane % U, -COLS)
    cols = jnp.arange(COLS, dtype=jnp.int32)
    spread_to = (place[None, :] + h_to[:, None] * U).reshape(-1)
    perm_to = (cols[:, None] == spread_to[None, :]).astype(BF)
    perm_from = (cols[None, None, :] == (place[None, :] + h_from[:, None] * U)[:, :, None]).astype(BF)
    piece = jax.ShapeDtypeStruct((NC, ROWS // 4, 384), BF)
    x_out = pl.pallas_call(
        x_kernel,
        out_shape=[piece] * NZ,
        in_specs=[SM] + [VM] * 7 + [HBM] + [VM] * 2,
        out_specs=[VM] * NZ,
        scratch_shapes=[
            pltpu.VMEM((8, ROWS, COLS), BF),
            pltpu.VMEM((ROWS, COLS), BF),
            pltpu.SemaphoreType.DMA((8,)),
        ],
        compiler_params=params(12),
        name="beta_product",
    )(slots.reshape(-1), *[blocks[k] for k in ARRIVAL], beta_values[0].reshape(6, 768, 128), perm_to)
    direct = [x_out[0]] + [send_step(x_out[k], k) for k in range(1, NZ)]
    x_parts = direct + [flip_core(a) for a in direct[:3]]
    a_own = pl.pallas_call(
        stack_kernel,
        out_shape=jax.ShapeDtypeStruct((NZ - 1, ROWS + 8, COLS), BF),
        in_specs=[HBM] * NZ,
        out_specs=HBM,
        scratch_shapes=[pltpu.SemaphoreType.DMA((NZ - 1,))],
        compiler_params=params(4),
        name="stack_tiles",
    )(x_out[0], *a_near)

    size = ROWS * NH
    part = jax.ShapeDtypeStruct((size // 4, 384), BF)
    by_label = [x_parts[i % 2 * NZ + i // 2] for i in range(FIRST)]
    a_pair = (a_own, flip_core(a_own))
    total = jax.ShapeDtypeStruct((size * NY, 128), F32)
    acc, done = pl.pallas_call(
        first_kernel,
        out_shape=[total, jax.ShapeDtypeStruct((8, 128), F32)],
        in_specs=[SM] + [HBM] * (3 + FIRST),
        out_specs=[VM] * 2,
        scratch_shapes=product_scratch(FIRST),
        compiler_params=params(16),
        cost_estimate=cost(6),
        name="alpha_product_first",
    )(y.reshape(1), *a_pair, *by_label, a_far)
    farthest, a_far, done = lax.optimization_barrier((direct[3], a_far, done))
    _, own, s1, s2, s3 = pl.pallas_call(
        last_kernel,
        out_shape=[total, jax.ShapeDtypeStruct((size, 128), F32), part, part, part],
        in_specs=[SM] + [HBM] * (2 + NH - FIRST) + [VM] * 2,
        out_specs=[VM] * 5,
        input_output_aliases={3 + NH - FIRST: 0},
        scratch_shapes=product_scratch(NH - FIRST),
        compiler_params=params(16),
        name="alpha_product_last",
    )(y.reshape(1), a_far, flip_core(a_far), farthest, flip_core(farthest), acc, done)
    r2, r1, r3 = shift_y(s2, 2), shift_y(s1, 1), shift_y(s3, 3)

    y_out = pl.pallas_call(
        y_kernel,
        out_shape=[jax.ShapeDtypeStruct((NZ, ROWS // 4, 384), BF)] * NC
        + [jax.ShapeDtypeStruct((NY * G, U, ROWS), BF)],
        in_specs=[SM] + [VM] * 5,
        out_specs=[VM] * (NC + 1),
        scratch_shapes=[pltpu.VMEM((size, 128), F32)],
        compiler_params=params(12),
        name="y_sum",
    )(h_to, r2, own, r1, r3, jnp.eye(128, dtype=BF))
    came = flip_core(y_out[1])
    mirrored = lax.all_to_all(y_out[NC], ("y", "zl", "x"), split_axis=0, concat_axis=0, tiled=True)
    pairs = pl.pallas_call(
        pair_kernel,
        out_shape=[piece] * NZ,
        in_specs=[HBM] * 2,
        out_specs=[HBM] * NZ,
        scratch_shapes=[pltpu.SemaphoreType.DMA((2 * NZ,))],
        compiler_params=params(4),
        name="pair_pieces",
    )(y_out[0], came)
    d_parts = [pairs[0]] + [send_step(pairs[k], k) for k in range(1, NZ)]
    out = pl.pallas_call(
        out_kernel,
        out_shape=jax.ShapeDtypeStruct((ROWS, COLS), F32),
        in_specs=[VM] * (NZ + 3),
        out_specs=VM,
        compiler_params=params(12),
        name="combine",
    )(d_parts[3], *d_parts[:3], mirrored.reshape(NY, ROWS, ROWS), perm_from, gaps.reshape(ROWS, COLS))
    return out.reshape(gaps.shape)


def solution(mesh):
    fine = Mesh(mesh.devices.reshape(NY, NZ, NC, NL, NX), ("y", "zh", "core", "zl", "x"))
    row, col = ("y", "zh", "core"), ("zl", "x")
    placed = (
        P(None, row, col),
        P(None, col, None, None, None),
        P(None, col, None),
        P(None, None, row, None, None, None),
        P(None, None, row, None),
        P(None, row, col),
    )
    return jax.shard_map(
        per_device, mesh=fine, in_specs=placed, out_specs=P(None, row, col), check_vma=False
    )
```
